256 devices in a mesh: section: 8 (over z), seq: 32 (over y, x, core).
Axes of the slice: x: 4, y: 4, z: 8, core: 2. Of those that a mesh axis runs over, the one named last changes fastest.
Arguments:
- stream_in: bfloat16 [2, 4096, 4096], P(None, 'seq'), may hold values from -30 to 30
- norm_gain: float32 [8, 4096], P('section'), may hold values from 0.25 to 1.75
- proj_weight: bfloat16 [8, 32, 4, 128, 128], P('section'), may hold values from -0.5 to 0.5
Outputs:
- streams: bfloat16 [8, 2, 4096, 4096], P('section', None, 'seq')
The draws below stay inside these ranges and needn't reach their ends.
All inputs are finite; a program needn't handle non-finite values.
Results may differ from the reference program's by a relative error of at most 0.014.
Values may be sent and summed in bfloat16 or wider, within the bound.
No kernel may reach another device: no remote copies, remote signals or barrier semaphores. Data moves between devices by JAX's collectives and lax.ppermute only.
A program may use at most 64 MiB of HBM per device.

```python
import math
import jax
import jax.numpy as jnp
from jax import lax

HEADS = 32
HEAD = 128
WIDTH = 4096
TOK_DEV = 128
MICRO = 2
LAYERS = 8
SEQLEN = 4096


def draw_stream_in(key, part):
    key_base, key_cols, key_rows = jax.random.split(jax.random.fold_in(key, 17), 3)
    array_shape = (MICRO, SEQLEN, WIDTH)
    base_draw = jnp.clip(jax.random.normal(key_base, array_shape, jnp.float32), -5.0, 5.0)
    column_scale = jnp.exp(jax.random.uniform(key_cols, (WIDTH,), jnp.float32, math.log(0.3), math.log(3.0)))
    row_scale = jnp.exp(jax.random.uniform(key_rows, (MICRO, SEQLEN, 1), jnp.float32, math.log(0.5), math.log(2.0)))
    return (base_draw * column_scale * row_scale).astype(jnp.bfloat16)


def levels(key, extent, pieces, smallest, largest):
    level, own = 1.0, jax.random.fold_in(key, 6)
    for position, parts in pieces:
        draws = jnp.exp(jax.random.uniform(jax.random.fold_in(own, position), (parts,), jnp.float32, smallest / len(pieces), largest / len(pieces)))
        level = level * jnp.repeat(draws, extent[position] // parts).reshape([-1 if axis == position else 1 for axis in range(len(extent))])
    return level


def bell_draw(own_key, dims, deviation, reach, cuts=(), dtype=jnp.bfloat16):
    level = levels(own_key, dims, cuts, -0.22, 0.18) if cuts else 1.0
    result = jax.random.normal(own_key, dims, jnp.float32) * deviation * level
    return jnp.minimum(jnp.maximum(result, -reach), reach).astype(dtype)


def setup_inputs(seed: int = 0) -> dict:
    streams_of = jax.random.split(jax.random.key(seed), 4)
    stream_in = draw_stream_in(jax.random.fold_in(streams_of[3], 71), 0)
    norm_gain = jnp.clip(1.0 + 0.15 * jax.random.normal(streams_of[1], (LAYERS, WIDTH), jnp.float32), 0.25, 1.75)
    proj_weight = bell_draw(streams_of[2], (LAYERS, HEADS, 4, HEAD, HEAD), HEAD ** -0.5, 0.5, ((0, 8),))
    return dict(stream_in=stream_in, norm_gain=norm_gain, proj_weight=proj_weight)


epsilon = 1e-05

def rms_scale(values):
    return lax.rsqrt(lax.optimization_barrier(jnp.mean(values * values, axis=-1, keepdims=True)) + epsilon)

def round_back(values):
    return lax.optimization_barrier(values.astype(jnp.bfloat16)).astype(jnp.float32)

def layer_apply(stream, gain, weights):
    total_rows, width = stream.shape
    head_count, head_size = (weights.shape[0], weights.shape[2])
    wide = stream.astype(jnp.float32)
    normed = round_back(wide * rms_scale(wide) * gain)
    split = normed.reshape(total_rows, head_count, head_size)
    mixed = jnp.einsum('thc,hjcd->jthd', split, weights[:, :3].astype(jnp.float32))
    blocks = total_rows // TOK_DEV
    query = round_back(jax.nn.silu(mixed[0])).reshape(blocks, TOK_DEV, head_count, head_size)
    key_part = round_back(jax.nn.silu(mixed[1])).reshape(blocks, TOK_DEV, head_count, head_size)
    value_part = round_back(mixed[2]).reshape(blocks, TOK_DEV, head_count, head_size)
    states = jnp.einsum('bthc,bthd->bhcd', key_part, value_part)
    running = jnp.cumsum(states, axis=0)
    carried = jnp.concatenate([jnp.zeros_like(states[:1]), running[:-1]], axis=0)
    carried_low = round_back(carried)
    inter = jnp.einsum('bthc,bhcd->bthd', query, carried_low)
    scores = jnp.einsum('bthc,bshc->bhts', query, key_part)
    causal = lax.broadcasted_iota(jnp.int32, (TOK_DEV, TOK_DEV), 0) >= lax.broadcasted_iota(jnp.int32, (TOK_DEV, TOK_DEV), 1)
    scores = round_back(jnp.where(causal[None, None], scores, jnp.zeros_like(scores)))
    intra = jnp.einsum('bhts,bshd->bthd', scores, value_part)
    attn = inter + intra
    head_out = round_back(attn * rms_scale(attn)).reshape(total_rows, head_count, head_size)
    projected = jnp.einsum('thc,hcd->thd', head_out, weights[:, 3].astype(jnp.float32))
    return (wide + projected.reshape(total_rows, width)).astype(jnp.bfloat16)

def reference(stream_in, norm_gain, proj_weight):
    per_layer = [[] for layer_index in range(LAYERS)]
    for micro_index in range(MICRO):
        current = stream_in[micro_index]
        for layer_index in range(LAYERS):
            current = layer_apply(current, norm_gain[layer_index], proj_weight[layer_index])
            per_layer[layer_index].append(current)
    return jnp.stack([jnp.stack(layer_list) for layer_list in per_layer])
```

```python
import functools

import jax
import jax.numpy as jnp
from jax import lax
from jax.experimental import pallas as pl
from jax.experimental.pallas import tpu as pltpu
from jax.sharding import PartitionSpec as P

epsilon = 1e-05
LAYERS = 8
SEQ = 32
MICRO = 2
BLOCK = 128
HEAD = 128
WIDTH = 4096
STEP = 4
EXTRA = 16
NT = (((1,), (1,)), ((), ()))
TN = (((0,), (0,)), ((), ()))
VM = pl.BlockSpec(memory_space=pltpu.VMEM)
SM = pl.BlockSpec(memory_space=pltpu.SMEM)
ANY = pl.BlockSpec(memory_space=pl.ANY)


def dot(a, b):
    return jnp.dot(a, b, preferred_element_type=jnp.float32)


def pack_kernel(sec_ref, x_ref, packed_ref):
    micro = lax.rem(sec_ref[0], MICRO)
    total = jnp.zeros((BLOCK, HEAD), jnp.float32)
    for h in range(SEQ):
        piece = x_ref[micro, :, h * HEAD : (h + 1) * HEAD]
        packed_ref[h, :BLOCK, :] = piece
        wide = piece.astype(jnp.float32)
        total = total + wide * wide
    row = jnp.broadcast_to(jnp.sum(total, axis=1, keepdims=True), (BLOCK, HEAD)).T[:1]
    high = row.astype(jnp.bfloat16)
    rest = row - high.astype(jnp.float32)
    middle = rest.astype(jnp.bfloat16)
    low = (rest - middle.astype(jnp.float32)).astype(jnp.bfloat16)
    rows = lax.broadcasted_iota(jnp.int32, (EXTRA, HEAD), 0)
    wide_rows = [jnp.broadcast_to(p.astype(jnp.float32), (EXTRA, HEAD)) for p in (high, middle, low)]
    tail = jnp.where(rows == 0, wide_rows[0], jnp.where(rows == 1, wide_rows[1], jnp.where(rows == 2, wide_rows[2], 0.0)))
    tail = tail.astype(jnp.bfloat16)
    for h in range(SEQ):
        packed_ref[h, BLOCK:, :] = tail


def pack(section, stream):
    return pl.pallas_call(
        pack_kernel,
        in_specs=[SM, VM],
        out_specs=VM,
        out_shape=jax.ShapeDtypeStruct((SEQ, BLOCK + EXTRA, HEAD), jnp.bfloat16),
        compiler_params=pltpu.CompilerParams(vmem_limit_bytes=16 << 20),
    )(section, stream)


def layer_kernel(layer, part_count, sec_ref, *refs):
    part_refs = refs[:part_count]
    w_ref, x_ref = refs[part_count : part_count + 2]
    xo_ref, ss_ref, own_ref, far_ref, scale_ref, sums_ref, copy_sem = refs[part_count + 4 :]
    if part_count:
        total = part_refs[0][...]
        for ref in part_refs[1:]:
            total = total + ref[...]
    else:
        tail = x_ref[:, BLOCK:, :].astype(jnp.float32)
        total = tail[:, 0, :] + tail[:, 1, :] + tail[:, 2, :]
    half_scale = 0.5 * lax.rsqrt(total * (1.0 / WIDTH) + epsilon)
    scale_ref[...] = jnp.concatenate([half_scale] * (BLOCK // SEQ), axis=0).T
    sums_ref[...] = jnp.zeros_like(sums_ref)
    wqkv = jnp.concatenate([w_ref[layer, 0], w_ref[layer, 1], w_ref[layer, 2]], axis=1)
    wo = w_ref[layer, 3]
    lanes = lax.broadcasted_iota(jnp.int32, (BLOCK, BLOCK), 1)
    rows = lax.broadcasted_iota(jnp.int32, (BLOCK, BLOCK), 0)
    causal = rows >= lanes

    def step(index, carried):
        first = index * STEP
        xs = [x_ref[first + n, :BLOCK, :] for n in range(STEP)]
        scales = [jnp.sum(jnp.where(lanes == first + n, scale_ref[...], 0.0), axis=1, keepdims=True) for n in range(STEP)]
        us = [dot(x, wqkv) for x in xs]
        qs, ks, vs = [], [], []
        for n in range(STEP):
            s = scales[n]
            h = us[n][:, : 2 * HEAD] * s
            qk = (h * jnp.tanh(h) + h).astype(jnp.bfloat16)
            qs.append(qk[:, :HEAD])
            ks.append(qk[:, HEAD:])
            vs.append((us[n][:, 2 * HEAD :] * (2.0 * s)).astype(jnp.bfloat16))
        states = [lax.dot_general(ks[n], vs[n], TN, preferred_element_type=jnp.float32) for n in range(STEP)]
        scores = [
            jnp.where(causal, lax.dot_general(qs[n], ks[n], NT, preferred_element_type=jnp.float32), 0.0).astype(jnp.bfloat16)
            for n in range(STEP)
        ]
        attns = []
        for n in range(STEP):
            attns.append(dot(scores[n], vs[n]) + dot(qs[n], carried.astype(jnp.bfloat16)))
            carried = carried + states[n]
        outs = []
        for n in range(STEP):
            a = attns[n]
            scale = lax.rsqrt(jnp.sum(a * a, axis=1, keepdims=True) * (1.0 / HEAD) + epsilon)
            outs.append(dot((a * scale).astype(jnp.bfloat16), wo))
        sums = sums_ref[...]
        for n in range(STEP):
            new = (xs[n].astype(jnp.float32) + outs[n]).astype(jnp.bfloat16)
            xo_ref[first + n] = new
            wide = new.astype(jnp.float32)
            sums = jnp.where(lanes == first + n, jnp.sum(wide * wide, axis=1, keepdims=True), sums)
        sums_ref[...] = sums
        return carried

    lax.fori_loop(0, SEQ // STEP, step, jnp.zeros((HEAD, HEAD), jnp.float32))
    ss_ref[...] = sums_ref[...].T[:SEQ]

    half = SEQ // 2
    section = sec_ref[0]

    def keep(source, target):
        copy = pltpu.make_async_copy(source, target, copy_sem)
        copy.start()
        copy.wait()

    @pl.when(section == layer)
    def _():
        keep(xo_ref, own_ref)

    @pl.when(section == (layer - 1) % LAYERS)
    def _():
        keep(xo_ref.at[:half], far_ref.at[0])

    @pl.when(section == (layer + 1) % LAYERS)
    def _():
        keep(xo_ref.at[half:], far_ref.at[1])


def run_layer(layer, section, parts, weights, x, own, far):
    n = len(parts)
    stream = jax.ShapeDtypeStruct((SEQ, BLOCK, HEAD), jnp.bfloat16)
    return pl.pallas_call(
        functools.partial(layer_kernel, layer, n),
        in_specs=[SM] + [VM] * (n + 2) + [ANY, ANY],
        out_specs=[VM, VM, ANY, ANY],
        out_shape=[
            stream,
            jax.ShapeDtypeStruct((SEQ, BLOCK), jnp.float32),
            stream,
            jax.ShapeDtypeStruct((2, SEQ // 2, BLOCK, HEAD), jnp.bfloat16),
        ],
        scratch_shapes=[
            pltpu.VMEM((BLOCK, BLOCK), jnp.float32),
            pltpu.VMEM((BLOCK, BLOCK), jnp.float32),
            pltpu.SemaphoreType.DMA,
        ],
        input_output_aliases={n + 3: 2, n + 4: 3},
        compiler_params=pltpu.CompilerParams(vmem_limit_bytes=24 << 20),
        cost_estimate=pl.CostEstimate(flops=1_100_000_000, bytes_accessed=2 << 20, transcendentals=1 << 20),
    )(section, *parts, weights, x, own, far)


def unpack_kernel(sec_ref, own_ref, other_ref, out_ref):
    micro = lax.rem(sec_ref[0], MICRO)
    for h in range(SEQ):
        out_ref[0, micro, :, h * HEAD : (h + 1) * HEAD] = own_ref[h]
        out_ref[0, 1 - micro, :, h * HEAD : (h + 1) * HEAD] = other_ref[h]


def unpack(section, own, other):
    return pl.pallas_call(
        unpack_kernel,
        in_specs=[SM, VM, VM],
        out_specs=VM,
        out_shape=jax.ShapeDtypeStruct((1, MICRO, BLOCK, WIDTH), jnp.bfloat16),
        compiler_params=pltpu.CompilerParams(vmem_limit_bytes=16 << 20),
    )(section, own, other)


def index_of(y, x, c):
    return ((y % 4) * 4 + x % 4) * 2 + c


def shifted(value, dy, dx, dc):
    pairs = [
        (index_of(y, x, c), index_of(y + dy, x + dx, (c + dc) % 2)) for y in range(4) for x in range(4) for c in range(2)
    ]
    return lax.ppermute(value, "seq", pairs)


def sum_parts(value):
    value = value + shifted(value, 0, 0, 1)
    value = value + shifted(value, 0, 1, 0) + shifted(value, 0, 2, 0) + shifted(value, 0, 3, 0)
    return [value] + [shifted(value, d, 0, 0) for d in (1, 2, 3)]


def around(value, by):
    sections = lax.axis_size("section")
    return lax.ppermute(value, "section", [(i, (i + by) % sections) for i in range(sections)])


def on_device(stream_in, norm_gain, proj_weight):
    head = lax.axis_index("seq")
    section = lax.axis_index("section").astype(jnp.int32).reshape(1)
    own_weights = lax.dynamic_index_in_dim(proj_weight[0], head, 0, keepdims=False)
    gain = lax.dynamic_slice_in_dim(norm_gain[0], head * HEAD, HEAD, 0)
    gains = jnp.concatenate([jnp.broadcast_to(gain, (3, HEAD)), jnp.ones((1, HEAD), jnp.float32)], axis=0)
    folded = (own_weights.astype(jnp.float32) * gains[:, :, None]).astype(jnp.bfloat16)
    weights = lax.all_to_all(jnp.broadcast_to(folded[None], (LAYERS,) + folded.shape), "section", 0, 0, tiled=True)

    x = lax.all_to_all(pack(section, stream_in), "seq", split_axis=0, concat_axis=0, tiled=True)
    own = jnp.zeros((SEQ, BLOCK, HEAD), jnp.bfloat16)
    far = jnp.zeros((2, SEQ // 2, BLOCK, HEAD), jnp.bfloat16)
    parts = []
    for layer in range(LAYERS):
        x, sums, own, far = run_layer(layer, section, parts, weights, x, own, far)
        if layer < LAYERS - 1:
            parts = sum_parts(sums)
    low = around(far[0], 1)
    high = around(far[1], -1)
    own = lax.all_to_all(own, "seq", split_axis=0, concat_axis=0, tiled=True)
    other = lax.all_to_all(jnp.concatenate([low, high], axis=0), "seq", split_axis=0, concat_axis=0, tiled=True)
    return unpack(section, own, other)


def solution(mesh):
    in_specs = (P(None, "seq", None), P("section", None), P("section", None, None, None, None))
    out_specs = P("section", None, "seq", None)
    return jax.shard_map(on_device, mesh=mesh, in_specs=in_specs, out_specs=out_specs, check_vma=False)
```

```python
import functools

import jax
import jax.numpy as jnp
from jax import lax
from jax.experimental import pallas as pl
from jax.experimental.pallas import tpu as pltpu
from jax.sharding import PartitionSpec as P

epsilon = 1e-05
LAYERS = 8
SEQ = 32
MICRO = 2
BLOCK = 128
HEAD = 128
WIDTH = 4096
STEP = 4
EXTRA = 16
CHIPS = SEQ // 2
NT = (((1,), (1,)), ((), ()))
VM = pl.BlockSpec(memory_space=pltpu.VMEM)
SM = pl.BlockSpec(memory_space=pltpu.SMEM)
ANY = pl.BlockSpec(memory_space=pl.ANY)


def dot(a, b):
    return jnp.dot(a, b, preferred_element_type=jnp.float32)


def pack_kernel(sec_ref, x_ref, packed_ref):
    micro = lax.rem(sec_ref[0], MICRO)
    total = jnp.zeros((BLOCK, HEAD), jnp.float32)
    for h in range(SEQ):
        piece = x_ref[micro, :, h * HEAD : (h + 1) * HEAD]
        packed_ref[h, :BLOCK, :] = piece
        wide = piece.astype(jnp.float32)
        total = total + wide * wide
    row = jnp.broadcast_to(jnp.sum(total, axis=1, keepdims=True), (BLOCK, HEAD)).T[:1]
    high = row.astype(jnp.bfloat16)
    rest = row - high.astype(jnp.float32)
    middle = rest.astype(jnp.bfloat16)
    low = (rest - middle.astype(jnp.float32)).astype(jnp.bfloat16)
    rows = lax.broadcasted_iota(jnp.int32, (EXTRA, HEAD), 0)
    wide_rows = [jnp.broadcast_to(p.astype(jnp.float32), (EXTRA, HEAD)) for p in (high, middle, low)]
    tail = jnp.where(rows == 0, wide_rows[0], jnp.where(rows == 1, wide_rows[1], jnp.where(rows == 2, wide_rows[2], 0.0)))
    tail = tail.astype(jnp.bfloat16)
    for h in range(SEQ):
        packed_ref[h, BLOCK:, :] = tail


def pack(section, stream):
    return pl.pallas_call(
        pack_kernel,
        in_specs=[SM, VM],
        out_specs=VM,
        out_shape=jax.ShapeDtypeStruct((SEQ, BLOCK + EXTRA, HEAD), jnp.bfloat16),
        compiler_params=pltpu.CompilerParams(vmem_limit_bytes=16 << 20),
    )(section, stream)


def layer_kernel(layer, first_layer, sec_ref, *refs):
    sum_refs = () if first_layer else refs[:1]
    w_ref, x_ref = refs[len(sum_refs) : len(sum_refs) + 2]
    xo_ref, ss_ref, own_ref, far_ref, column_ref, row_ref, q_ref, k_ref, v_ref, copy_sem = refs[len(sum_refs) + 4 :]
    if first_layer:
        tail = x_ref[:, BLOCK:, :].astype(jnp.float32)
        total = tail[:, 0, :] + tail[:, 1, :] + tail[:, 2, :]
    else:
        total = sum_refs[0][0].astype(jnp.float32)
        for n in range(1, CHIPS):
            total = total + sum_refs[0][n].astype(jnp.float32)
    half_scale = 0.5 * lax.rsqrt(total * (1.0 / WIDTH) + epsilon)
    row_ref[...] = half_scale
    column_ref[...] = jnp.concatenate([half_scale] * (BLOCK // SEQ), axis=0).T
    wqv = jnp.concatenate([w_ref[layer, 0], w_ref[layer, 2]], axis=1)
    wk = w_ref[layer, 1]
    wo = w_ref[layer, 3]
    lanes = lax.broadcasted_iota(jnp.int32, (BLOCK, BLOCK), 1)
    rows = lax.broadcasted_iota(jnp.int32, (BLOCK, BLOCK), 0)
    causal = rows >= lanes
    ones = jnp.ones((HEAD, HEAD), jnp.bfloat16)

    def front(index, slot):
        first = index * STEP
        for n in range(STEP):
            x = x_ref[first + n, :BLOCK, :]
            s = jnp.sum(jnp.where(lanes == first + n, column_ref[...], 0.0), axis=1, keepdims=True)
            u = dot(x, wqv)
            h = u[:, :HEAD] * s
            q_ref[slot, n] = (h * jnp.tanh(h) + h).astype(jnp.bfloat16)
            v_ref[slot, n] = (u[:, HEAD:] * (2.0 * s)).astype(jnp.bfloat16)
            h = lax.dot_general(wk, x, NT, preferred_element_type=jnp.float32) * row_ref[pl.ds(first + n, 1), :]
            k_ref[slot, n] = (h * jnp.tanh(h) + h).astype(jnp.bfloat16)

    def back(index, slot, carried):
        first = index * STEP
        qs = [q_ref[slot, n] for n in range(STEP)]
        ks = [k_ref[slot, n] for n in range(STEP)]
        vs = [v_ref[slot, n] for n in range(STEP)]
        states = [dot(ks[n], vs[n]) for n in range(STEP)]
        scores = [jnp.where(causal, dot(qs[n], ks[n]), 0.0).astype(jnp.bfloat16) for n in range(STEP)]
        attns = []
        for n in range(STEP):
            attns.append(dot(scores[n], vs[n]) + dot(qs[n], carried.astype(jnp.bfloat16)))
            carried = carried + states[n]
        squares = [dot((a * a).astype(jnp.bfloat16), ones) for a in attns]
        outs = [
            dot((attns[n] * lax.rsqrt(squares[n] * (1.0 / HEAD) + epsilon)).astype(jnp.bfloat16), wo) for n in range(STEP)
        ]
        for n in range(STEP):
            new = (x_ref[first + n, :BLOCK, :].astype(jnp.float32) + outs[n]).astype(jnp.bfloat16)
            xo_ref[first + n] = new
            wide = new.astype(jnp.float32)
            row = lax.dot_general(ones[:8], (wide * wide).astype(jnp.bfloat16), NT, preferred_element_type=jnp.float32)
            ss_ref[pl.ds(first + n, 1), :] = row[:1]
        return carried

    steps = SEQ // STEP
    front(0, 0)

    def step(index, carried):
        slot = lax.rem(index, 2)
        carried = back(index - 1, 1 - slot, carried)
        front(index, slot)
        return carried

    carried = lax.fori_loop(1, steps, step, jnp.zeros((HEAD, HEAD), jnp.float32))
    back(steps - 1, (steps - 1) % 2, carried)

    half = SEQ // 2
    section = sec_ref[0]

    def keep(source, target):
        copy = pltpu.make_async_copy(source, target, copy_sem)
        copy.start()
        copy.wait()

    @pl.when(section == layer)
    def _():
        keep(xo_ref, own_ref)

    @pl.when(section == (layer - 1) % LAYERS)
    def _():
        keep(xo_ref.at[:half], far_ref.at[0])

    @pl.when(section == (layer + 1) % LAYERS)
    def _():
        keep(xo_ref.at[half:], far_ref.at[1])


def run_layer(layer, section, sums, weights, x, own, far):
    n = 0 if sums is None else 1
    stream = jax.ShapeDtypeStruct((SEQ, BLOCK, HEAD), jnp.bfloat16)
    tile = pltpu.VMEM((2, STEP, BLOCK, HEAD), jnp.bfloat16)
    return pl.pallas_call(
        functools.partial(layer_kernel, layer, sums is None),
        in_specs=[SM] + [VM] * (n + 2) + [ANY, ANY],
        out_specs=[VM, VM, ANY, ANY],
        out_shape=[
            stream,
            jax.ShapeDtypeStruct((SEQ, BLOCK), jnp.float32),
            stream,
            jax.ShapeDtypeStruct((2, SEQ // 2, BLOCK, HEAD), jnp.bfloat16),
        ],
        scratch_shapes=[
            pltpu.VMEM((BLOCK, BLOCK), jnp.float32),
            pltpu.VMEM((SEQ, BLOCK), jnp.float32),
            tile,
            tile,
            tile,
            pltpu.SemaphoreType.DMA,
        ],
        input_output_aliases={n + 3: 2, n + 4: 3},
        compiler_params=pltpu.CompilerParams(vmem_limit_bytes=24 << 20),
        cost_estimate=pl.CostEstimate(flops=1_100_000_000, bytes_accessed=2 << 20, transcendentals=1 << 20),
    )(section, *(() if sums is None else (sums,)), weights, x, own, far)


def order_kernel(sec_ref, *refs):
    out_ref = refs[-1]
    for by in range(LAYERS):
        out_ref[lax.rem(sec_ref[0] + LAYERS - by, LAYERS)] = refs[by][...]


def gather_weights(section, own):
    pieces = [own] + [around(own, by) for by in (4, 3, 5, 2, 6, 1, 7)]
    pieces = [pieces[i] for i in (0, 6, 4, 2, 1, 3, 5, 7)]
    return pl.pallas_call(
        order_kernel,
        in_specs=[SM] + [VM] * LAYERS,
        out_specs=VM,
        out_shape=jax.ShapeDtypeStruct((LAYERS,) + own.shape, own.dtype),
        compiler_params=pltpu.CompilerParams(vmem_limit_bytes=16 << 20),
    )(section, *pieces)


def unpack_kernel(sec_ref, own_ref, other_ref, out_ref):
    micro = lax.rem(sec_ref[0], MICRO)
    for h in range(SEQ):
        out_ref[0, micro, :, h * HEAD : (h + 1) * HEAD] = own_ref[h]
        out_ref[0, 1 - micro, :, h * HEAD : (h + 1) * HEAD] = other_ref[h]


def unpack(section, own, other):
    return pl.pallas_call(
        unpack_kernel,
        in_specs=[SM, VM, VM],
        out_specs=VM,
        out_shape=jax.ShapeDtypeStruct((1, MICRO, BLOCK, WIDTH), jnp.bfloat16),
        compiler_params=pltpu.CompilerParams(vmem_limit_bytes=16 << 20),
    )(section, own, other)


def spread_sums(value):
    swap = [(i, i ^ 1) for i in range(SEQ)]
    value = (value + lax.ppermute(value, "seq", swap)).astype(jnp.bfloat16)
    groups = [[2 * chip + core for chip in range(CHIPS)] for core in range(2)]
    copies = jnp.broadcast_to(value[None], (CHIPS,) + value.shape)
    return lax.all_to_all(copies, "seq", 0, 0, tiled=True, axis_index_groups=groups)


def around(value, by):
    sections = lax.axis_size("section")
    return lax.ppermute(value, "section", [(i, (i + by) % sections) for i in range(sections)])


def on_device(stream_in, norm_gain, proj_weight):
    head = lax.axis_index("seq")
    section = lax.axis_index("section").astype(jnp.int32).reshape(1)
    own_weights = lax.dynamic_index_in_dim(proj_weight[0], head, 0, keepdims=False)
    gain = lax.dynamic_slice_in_dim(norm_gain[0], head * HEAD, HEAD, 0)
    gains = jnp.concatenate([jnp.broadcast_to(gain, (3, HEAD)), jnp.ones((1, HEAD), jnp.float32)], axis=0)
    folded = (own_weights.astype(jnp.float32) * gains[:, :, None])
    turned = jnp.where(lax.broadcasted_iota(jnp.int32, (4, 1, 1), 0) == 1, folded.transpose(0, 2, 1), folded)
    folded = turned.astype(jnp.bfloat16)
    weights = gather_weights(section, folded)

    x = lax.all_to_all(pack(section, stream_in), "seq", split_axis=0, concat_axis=0, tiled=True)
    own = jnp.zeros((SEQ, BLOCK, HEAD), jnp.bfloat16)
    far = jnp.zeros((2, SEQ // 2, BLOCK, HEAD), jnp.bfloat16)
    sums = None
    for layer in range(LAYERS):
        x, sums, own, far = run_layer(layer, section, sums, weights, x, own, far)
        if layer < LAYERS - 1:
            sums = spread_sums(sums)
    low = around(far[0], 1)
    high = around(far[1], -1)
    own = lax.all_to_all(own, "seq", split_axis=0, concat_axis=0, tiled=True)
    other = lax.all_to_all(jnp.concatenate([low, high], axis=0), "seq", split_axis=0, concat_axis=0, tiled=True)
    return unpack(section, own, other)


def solution(mesh):
    in_specs = (P(None, "seq", None), P("section", None), P("section", None, None, None, None))
    out_specs = P("section", None, "seq", None)
    return jax.shard_map(on_device, mesh=mesh, in_specs=in_specs, out_specs=out_specs, check_vma=False)
```

```python
import functools

import jax
import jax.numpy as jnp
from jax import lax
from jax.experimental import pallas as pl
from jax.experimental.pallas import tpu as pltpu
from jax.sharding import PartitionSpec as P

epsilon = 1e-05
LAYERS = 8
SEQ = 32
MICRO = 2
BLOCK = 128
HEAD = 128
WIDTH = 4096
STEP = 4
EXTRA = 16
CHIPS = SEQ // 2
NT = (((1,), (1,)), ((), ()))
VM = pl.BlockSpec(memory_space=pltpu.VMEM)
SM = pl.BlockSpec(memory_space=pltpu.SMEM)
ANY = pl.BlockSpec(memory_space=pl.ANY)


def dot(a, b):
    return jnp.dot(a, b, preferred_element_type=jnp.float32)


def split_rows(row):
    high = row.astype(jnp.bfloat16)
    rest = row - high.astype(jnp.float32)
    middle = rest.astype(jnp.bfloat16)
    low = (rest - middle.astype(jnp.float32)).astype(jnp.bfloat16)
    rows = lax.broadcasted_iota(jnp.int32, (EXTRA, HEAD), 0)
    wide_rows = [jnp.broadcast_to(p.astype(jnp.float32), (EXTRA, HEAD)) for p in (high, middle, low)]
    tail = jnp.where(rows == 0, wide_rows[0], jnp.where(rows == 1, wide_rows[1], jnp.where(rows == 2, wide_rows[2], 0.0)))
    return tail.astype(jnp.bfloat16)


def split_squares(values):
    squares = values * values
    high = squares.astype(jnp.bfloat16)
    return jnp.concatenate([high, (squares - high.astype(jnp.float32)).astype(jnp.bfloat16)], axis=1)


def prepare_kernel(head_ref, weight_ref, gain_ref, out_ref, own_ref, copy_sem):
    head = head_ref[0]
    copy = pltpu.make_async_copy(weight_ref.at[0, head], own_ref, copy_sem)
    copy.start()
    gain = gain_ref[:, pl.ds(pl.multiple_of(head * HEAD, HEAD), HEAD)]
    out_ref[4 * HEAD :, :] = split_rows(gain)
    copy.wait()
    for n in range(4):
        piece = own_ref[n]
        if n == 1:
            piece = piece.astype(jnp.float32).T.astype(jnp.bfloat16)
        out_ref[n * HEAD : (n + 1) * HEAD, :] = piece


def prepare(head, proj_weight, norm_gain):
    return pl.pallas_call(
        prepare_kernel,
        in_specs=[SM, ANY, VM],
        out_specs=VM,
        out_shape=jax.ShapeDtypeStruct((4 * HEAD + EXTRA, HEAD), jnp.bfloat16),
        scratch_shapes=[pltpu.VMEM((4, HEAD, HEAD), jnp.bfloat16), pltpu.SemaphoreType.DMA],
        compiler_params=pltpu.CompilerParams(vmem_limit_bytes=16 << 20),
    )(head, proj_weight, norm_gain)


def pack_kernel(sec_ref, stream_ref, packed_ref, x_ref, copy_sem):
    copy = pltpu.make_async_copy(stream_ref.at[lax.rem(sec_ref[0], MICRO)], x_ref, copy_sem)
    copy.start()
    copy.wait()
    total = jnp.zeros((BLOCK, HEAD), jnp.float32)
    for h in range(SEQ):
        piece = x_ref[:, h * HEAD : (h + 1) * HEAD]
        packed_ref[h, :BLOCK, :] = piece
        wide = piece.astype(jnp.float32)
        total = total + wide * wide
    row = jnp.broadcast_to(jnp.sum(total, axis=1, keepdims=True), (BLOCK, HEAD)).T[:1]
    tail = split_rows(row)
    for h in range(SEQ):
        packed_ref[h, BLOCK:, :] = tail


def pack(section, stream):
    return pl.pallas_call(
        pack_kernel,
        in_specs=[SM, ANY],
        out_specs=VM,
        scratch_shapes=[pltpu.VMEM((BLOCK, WIDTH), jnp.bfloat16), pltpu.SemaphoreType.DMA],
        out_shape=jax.ShapeDtypeStruct((SEQ, BLOCK + EXTRA, HEAD), jnp.bfloat16),
        compiler_params=pltpu.CompilerParams(vmem_limit_bytes=16 << 20),
    )(section, stream)


def layer_kernel(layer, first_layer, sec_ref, *refs):
    sum_refs = () if first_layer else refs[:1]
    w_ref, x_ref = refs[len(sum_refs) : len(sum_refs) + 2]
    outputs = refs[2:] if first_layer else refs[5:]
    xo_ref, ss_ref, own_ref, far_ref, column_ref, q_ref, k_ref, v_ref, attn_ref, out_ref, copy_sem = outputs
    if first_layer:
        tail = x_ref[:, BLOCK:, :].astype(jnp.float32)
        total = tail[:, 0, :] + tail[:, 1, :] + tail[:, 2, :]
    else:
        total = sum_refs[0][0]
        for n in range(1, CHIPS):
            total = total + sum_refs[0][n]
    scale_rows = lax.rsqrt(total * (1.0 / WIDTH) + epsilon)
    column_ref[...] = jnp.concatenate([scale_rows] * (BLOCK // SEQ), axis=0).T
    wq, wk, wv, wo = [w_ref[layer, n * HEAD : (n + 1) * HEAD, :] for n in range(4)]
    wqv = jnp.concatenate([wq, wv], axis=1)
    gain_rows = w_ref[layer, 4 * HEAD :, :].astype(jnp.float32)
    gain = gain_rows[0:1] + gain_rows[1:2] + gain_rows[2:3]
    lanes = lax.broadcasted_iota(jnp.int32, (BLOCK, BLOCK), 1)
    rows = lax.broadcasted_iota(jnp.int32, (BLOCK, BLOCK), 0)
    causal = rows >= lanes
    ones_row = jnp.ones((8, 2 * HEAD), jnp.bfloat16)

    size = STEP * BLOCK

    def project(index):
        parts = []
        for n in range(STEP):
            block = index * STEP + n
            scale = jnp.sum(jnp.where(lanes == block, column_ref[...], 0.0), axis=1, keepdims=True)
            parts.append((x_ref[block, :BLOCK, :].astype(jnp.float32) * scale * gain).astype(jnp.bfloat16))
        normed = jnp.concatenate(parts, axis=0)
        return dot(normed, wqv), lax.dot_general(wk, normed, NT, preferred_element_type=jnp.float32)

    def activate(index, u, keys):
        for n in range(STEP):
            part = slice(n * BLOCK, (n + 1) * BLOCK)
            h = u[part, :HEAD] * 0.5
            q_ref[n] = (h * jnp.tanh(h) + h).astype(jnp.bfloat16)
            v_ref[n] = u[part, HEAD:].astype(jnp.bfloat16)
            h = keys[:, part] * 0.5
            k_ref[n] = (h * jnp.tanh(h) + h).astype(jnp.bfloat16)

    def finish(index):
        tile = pl.ds(index * STEP, STEP)
        x = x_ref[tile, :BLOCK, :].reshape(size, HEAD)
        new = (x.astype(jnp.float32) + out_ref[...]).astype(jnp.bfloat16)
        xo_ref[tile] = new.reshape(STEP, BLOCK, HEAD)
        wide = new.astype(jnp.float32)
        row = lax.dot_general(ones_row, split_squares(wide), NT, preferred_element_type=jnp.float32)
        for n in range(STEP):
            ss_ref[pl.ds(index * STEP + n, 1), :] = row[:1, n * BLOCK : (n + 1) * BLOCK]

    def advance(index, carried, stages):
        if 1 in stages:
            qs = [q_ref[n] for n in range(STEP)]
            ks = [k_ref[n] for n in range(STEP)]
            vs = [v_ref[n] for n in range(STEP)]
            scores = [jnp.where(causal, dot(qs[n], ks[n]), 0.0).astype(jnp.bfloat16) for n in range(STEP)]
        if 1 in stages:
            states = [dot(ks[n], vs[n]) for n in range(STEP)]
        if 2 in stages:
            attn = attn_ref[...]
            squares = jnp.sum(attn * attn, axis=1, keepdims=True)
        if 3 in stages:
            finish(index - 3)
        if 0 in stages:
            projected = project(index)
        if 1 in stages:
            for n in range(STEP):
                left = jnp.concatenate([scores[n], qs[n]], axis=1)
                part = dot(left, jnp.concatenate([vs[n], carried.astype(jnp.bfloat16)], axis=0))
                attn_ref[n * BLOCK : (n + 1) * BLOCK, :] = part
                carried = carried + states[n]
        if 2 in stages:
            scale = lax.rsqrt(squares * (1.0 / HEAD) + epsilon)
            out_ref[...] = dot((attn * scale).astype(jnp.bfloat16), wo)
        if 0 in stages:
            activate(index, *projected)
        return carried

    steps = SEQ // STEP
    carried = jnp.zeros((HEAD, HEAD), jnp.float32)
    for index in range(3):
        carried = advance(index, carried, range(index + 1))
    carried = lax.fori_loop(3, steps, lambda i, c: advance(i, c, range(4)), carried)
    for index in range(1, 4):
        carried = advance(steps + index - 1, carried, range(index, 4))

    half = SEQ // 2
    section = sec_ref[0]

    def keep(source, target):
        copy = pltpu.make_async_copy(source, target, copy_sem)
        copy.start()
        copy.wait()

    @pl.when(section == layer)
    def _():
        keep(xo_ref, own_ref)

    @pl.when(section == (layer - 1) % LAYERS)
    def _():
        keep(xo_ref.at[:half], far_ref.at[0])

    @pl.when(section == (layer + 1) % LAYERS)
    def _():
        keep(xo_ref.at[half:], far_ref.at[1])


def run_layer(layer, section, operands):
    first_layer = len(operands) == 2
    stream = jax.ShapeDtypeStruct((SEQ, BLOCK, HEAD), jnp.bfloat16)
    tile = pltpu.VMEM((STEP, BLOCK, HEAD), jnp.bfloat16)
    return pl.pallas_call(
        functools.partial(layer_kernel, layer, first_layer),
        in_specs=[SM, VM, VM] if first_layer else [SM, VM, VM, VM, ANY, ANY],
        out_specs=[VM, VM, ANY, ANY],
        out_shape=[
            stream,
            jax.ShapeDtypeStruct((SEQ, BLOCK), jnp.float32),
            stream,
            jax.ShapeDtypeStruct((2, SEQ // 2, BLOCK, HEAD), jnp.bfloat16),
        ],
        scratch_shapes=[
            pltpu.VMEM((BLOCK, BLOCK), jnp.float32),
            tile,
            tile,
            tile,
            pltpu.VMEM((STEP * BLOCK, HEAD), jnp.float32),
            pltpu.VMEM((STEP * BLOCK, HEAD), jnp.float32),
            pltpu.SemaphoreType.DMA,
        ],
        input_output_aliases={} if first_layer else {4: 2, 5: 3},
        compiler_params=pltpu.CompilerParams(vmem_limit_bytes=24 << 20),
        cost_estimate=pl.CostEstimate(flops=1_100_000_000, bytes_accessed=2 << 20, transcendentals=1 << 20),
    )(section, *operands)


def order_kernel(sec_ref, *refs):
    out_ref = refs[-1]
    for by in range(LAYERS):
        out_ref[lax.rem(sec_ref[0] + LAYERS - by, LAYERS)] = refs[by][...]


def order(section, pieces):
    return pl.pallas_call(
        order_kernel,
        in_specs=[SM] + [VM] * LAYERS,
        out_specs=VM,
        out_shape=jax.ShapeDtypeStruct((LAYERS,) + pieces[0].shape, pieces[0].dtype),
        compiler_params=pltpu.CompilerParams(vmem_limit_bytes=16 << 20),
    )(section, *pieces)


def gather_weights(section, own):
    up_two, down_two = around(own, 2), around(own, -2)
    up_one, down_one = around(own, 1), around(own, -1)
    up_four, up_three = around(up_two, 2), around(up_two, 1)
    down_three = around(down_two, -1)
    return order(section, [own, up_one, up_two, up_three, up_four, down_three, down_two, down_one])


def unpack_kernel(sec_ref, own_ref, other_ref, out_ref):
    micro = lax.rem(sec_ref[0], MICRO)
    for h in range(SEQ):
        out_ref[0, micro, :, h * HEAD : (h + 1) * HEAD] = own_ref[h]
        out_ref[0, 1 - micro, :, h * HEAD : (h + 1) * HEAD] = other_ref[h]


def unpack(section, own, other):
    return pl.pallas_call(
        unpack_kernel,
        in_specs=[SM, VM, VM],
        out_specs=VM,
        out_shape=jax.ShapeDtypeStruct((1, MICRO, BLOCK, WIDTH), jnp.bfloat16),
        compiler_params=pltpu.CompilerParams(vmem_limit_bytes=16 << 20),
    )(section, own, other)


def spread_sums(value):
    swap = [(i, i ^ 1) for i in range(SEQ)]
    value = value + lax.ppermute(value, "seq", swap)
    groups = [[2 * chip + core for chip in range(CHIPS)] for core in range(2)]
    copies = jnp.broadcast_to(value[None], (CHIPS,) + value.shape)
    return lax.all_to_all(copies, "seq", 0, 0, tiled=True, axis_index_groups=groups)


def around(value, by):
    sections = lax.axis_size("section")
    return lax.ppermute(value, "section", [(i, (i + by) % sections) for i in range(sections)])


def on_device(stream_in, norm_gain, proj_weight):
    head = lax.axis_index("seq")
    section = lax.axis_index("section").astype(jnp.int32).reshape(1)
    own_weights = prepare(head.astype(jnp.int32).reshape(1), proj_weight, norm_gain)
    weights = gather_weights(section, own_weights)

    x = lax.all_to_all(pack(section, stream_in), "seq", split_axis=0, concat_axis=0, tiled=True)
    x, sums, own, far = run_layer(0, section, (weights, x))
    for layer in range(1, LAYERS):
        x, sums, own, far = run_layer(layer, section, (spread_sums(sums), weights, x, own, far))
    low = around(far[0], 1)
    high = around(far[1], -1)
    own = lax.all_to_all(own, "seq", split_axis=0, concat_axis=0, tiled=True)
    other = lax.all_to_all(jnp.concatenate([low, high], axis=0), "seq", split_axis=0, concat_axis=0, tiled=True)
    return unpack(section, own, other)


def solution(mesh):
    in_specs = (P(None, "seq", None), P("section", None), P("section", None, None, None, None))
    out_specs = P("section", None, "seq", None)
    return jax.shard_map(on_device, mesh=mesh, in_specs=in_specs, out_specs=out_specs, check_vma=False)
```

```python
import functools

import jax
import jax.numpy as jnp
from jax import lax
from jax.experimental import pallas as pl
from jax.experimental.pallas import tpu as pltpu
from jax.sharding import PartitionSpec as P

epsilon = 1e-05
LAYERS = 8
SEQ = 32
MICRO = 2
BLOCK = 128
HEAD = 128
WIDTH = 4096
STEP = 4
EXTRA = 16
CHIPS = SEQ // 2
NT = (((1,), (1,)), ((), ()))
VM = pl.BlockSpec(memory_space=pltpu.VMEM)
SM = pl.BlockSpec(memory_space=pltpu.SMEM)
ANY = pl.BlockSpec(memory_space=pl.ANY)


def dot(a, b):
    return jnp.dot(a, b, preferred_element_type=jnp.float32)


def split_rows(row):
    high = row.astype(jnp.bfloat16)
    rest = row - high.astype(jnp.float32)
    middle = rest.astype(jnp.bfloat16)
    low = (rest - middle.astype(jnp.float32)).astype(jnp.bfloat16)
    rows = lax.broadcasted_iota(jnp.int32, (EXTRA, HEAD), 0)
    wide_rows = [jnp.broadcast_to(p.astype(jnp.float32), (EXTRA, HEAD)) for p in (high, middle, low)]
    tail = jnp.where(rows == 0, wide_rows[0], jnp.where(rows == 1, wide_rows[1], jnp.where(rows == 2, wide_rows[2], 0.0)))
    return tail.astype(jnp.bfloat16)


def split_squares(values):
    squares = values * values
    high = squares.astype(jnp.bfloat16)
    return jnp.concatenate([high, (squares - high.astype(jnp.float32)).astype(jnp.bfloat16)], axis=1)


def prepare_kernel(head_ref, weight_ref, gain_ref, out_ref, own_ref, copy_sem):
    head = head_ref[0]
    copy = pltpu.make_async_copy(weight_ref.at[0, head], own_ref, copy_sem)
    copy.start()
    gain = gain_ref[:, pl.ds(pl.multiple_of(head * HEAD, HEAD), HEAD)]
    out_ref[4 * HEAD :, :] = split_rows(gain)
    copy.wait()
    for n in range(4):
        piece = own_ref[n]
        if n == 1:
            piece = piece.astype(jnp.float32).T.astype(jnp.bfloat16)
        out_ref[n * HEAD : (n + 1) * HEAD, :] = piece


def prepare(head, proj_weight, norm_gain):
    return pl.pallas_call(
        prepare_kernel,
        in_specs=[SM, ANY, VM],
        out_specs=VM,
        out_shape=jax.ShapeDtypeStruct((4 * HEAD + EXTRA, HEAD), jnp.bfloat16),
        scratch_shapes=[pltpu.VMEM((4, HEAD, HEAD), jnp.bfloat16), pltpu.SemaphoreType.DMA],
        compiler_params=pltpu.CompilerParams(vmem_limit_bytes=63_000_000),
    )(head, proj_weight, norm_gain)


def pack_kernel(sec_ref, stream_ref, packed_ref, x_ref, copy_sem):
    copy = pltpu.make_async_copy(stream_ref.at[lax.rem(sec_ref[0], MICRO)], x_ref, copy_sem)
    copy.start()
    copy.wait()
    total = jnp.zeros((BLOCK, HEAD), jnp.float32)
    for h in range(SEQ):
        piece = x_ref[:, h * HEAD : (h + 1) * HEAD]
        packed_ref[h, :BLOCK, :] = piece
        wide = piece.astype(jnp.float32)
        total = total + wide * wide
    row = jnp.broadcast_to(jnp.sum(total, axis=1, keepdims=True), (BLOCK, HEAD)).T[:1]
    tail = split_rows(row)
    for h in range(SEQ):
        packed_ref[h, BLOCK:, :] = tail


def pack(section, stream):
    return pl.pallas_call(
        pack_kernel,
        in_specs=[SM, ANY],
        out_specs=VM,
        scratch_shapes=[pltpu.VMEM((BLOCK, WIDTH), jnp.bfloat16), pltpu.SemaphoreType.DMA],
        out_shape=jax.ShapeDtypeStruct((SEQ, BLOCK + EXTRA, HEAD), jnp.bfloat16),
        compiler_params=pltpu.CompilerParams(vmem_limit_bytes=66_000_000),
    )(section, stream)


def layer_kernel(layer, first_layer, sec_ref, *refs):
    sum_refs = () if first_layer else refs[:1]
    w_ref, x_ref = refs[len(sum_refs) : len(sum_refs) + 2]
    outputs = refs[2:] if first_layer else refs[5:]
    xo_ref, ss_ref, own_ref, far_ref, column_ref, q_ref, k_ref, v_ref, attn_ref, out_ref, copy_sem = outputs
    if first_layer:
        tail = x_ref[:, BLOCK:, :].astype(jnp.float32)
        total = tail[:, 0, :] + tail[:, 1, :] + tail[:, 2, :]
    else:
        total = sum_refs[0][0]
        for n in range(1, CHIPS):
            total = total + sum_refs[0][n]
    scale_rows = lax.rsqrt(total * (1.0 / WIDTH) + epsilon)
    column_ref[...] = jnp.concatenate([scale_rows] * (BLOCK // SEQ), axis=0).T
    wq, wk, wv, wo = [w_ref[layer, n * HEAD : (n + 1) * HEAD, :] for n in range(4)]
    wqv = jnp.concatenate([wq, wv], axis=1)
    gain_rows = w_ref[layer, 4 * HEAD :, :].astype(jnp.float32)
    gain = gain_rows[0:1] + gain_rows[1:2] + gain_rows[2:3]
    lanes = lax.broadcasted_iota(jnp.int32, (BLOCK, BLOCK), 1)
    rows = lax.broadcasted_iota(jnp.int32, (BLOCK, BLOCK), 0)
    causal = rows >= lanes
    ones_row = jnp.ones((8, 2 * HEAD), jnp.bfloat16)

    size = STEP * BLOCK

    def project(index):
        parts = []
        for n in range(STEP):
            block = index * STEP + n
            scale = jnp.sum(jnp.where(lanes == block, column_ref[...], 0.0), axis=1, keepdims=True)
            parts.append((x_ref[block, :BLOCK, :].astype(jnp.float32) * scale * gain).astype(jnp.bfloat16))
        normed = jnp.concatenate(parts, axis=0)
        return dot(normed, wqv), lax.dot_general(wk, normed, NT, preferred_element_type=jnp.float32)

    def activate(index, u, keys):
        for n in range(STEP):
            part = slice(n * BLOCK, (n + 1) * BLOCK)
            h = u[part, :HEAD] * 0.5
            q_ref[n] = (h * jnp.tanh(h) + h).astype(jnp.bfloat16)
            v_ref[n] = u[part, HEAD:].astype(jnp.bfloat16)
            h = keys[:, part] * 0.5
            k_ref[n] = (h * jnp.tanh(h) + h).astype(jnp.bfloat16)

    def finish(index):
        tile = pl.ds(index * STEP, STEP)
        x = x_ref[tile, :BLOCK, :].reshape(size, HEAD)
        new = (x.astype(jnp.float32) + out_ref[...]).astype(jnp.bfloat16)
        xo_ref[tile] = new.reshape(STEP, BLOCK, HEAD)
        wide = new.astype(jnp.float32)
        row = lax.dot_general(ones_row, split_squares(wide), NT, preferred_element_type=jnp.float32)
        for n in range(STEP):
            ss_ref[pl.ds(index * STEP + n, 1), :] = row[:1, n * BLOCK : (n + 1) * BLOCK]

    def advance(index, carried, stages):
        if 1 in stages:
            qs = [q_ref[n] for n in range(STEP)]
            ks = [k_ref[n] for n in range(STEP)]
            vs = [v_ref[n] for n in range(STEP)]
            scores = [jnp.where(causal, dot(qs[n], ks[n]), 0.0).astype(jnp.bfloat16) for n in range(STEP)]
        if 1 in stages:
            states = [dot(ks[n], vs[n]) for n in range(STEP)]
        if 2 in stages:
            attn = attn_ref[...]
            squares = jnp.sum(attn * attn, axis=1, keepdims=True)
        if 3 in stages:
            finish(index - 3)
        if 0 in stages:
            projected = project(index)
        if 1 in stages:
            for n in range(STEP):
                left = jnp.concatenate([scores[n], qs[n]], axis=1)
                part = dot(left, jnp.concatenate([vs[n], carried.astype(jnp.bfloat16)], axis=0))
                attn_ref[n * BLOCK : (n + 1) * BLOCK, :] = part
                carried = carried + states[n]
        if 2 in stages:
            scale = lax.rsqrt(squares * (1.0 / HEAD) + epsilon)
            out_ref[...] = dot((attn * scale).astype(jnp.bfloat16), wo)
        if 0 in stages:
            activate(index, *projected)
        return carried

    steps = SEQ // STEP
    carried = jnp.zeros((HEAD, HEAD), jnp.float32)
    for index in range(3):
        carried = advance(index, carried, range(index + 1))
    carried = lax.fori_loop(3, steps, lambda i, c: advance(i, c, range(4)), carried)
    for index in range(1, 4):
        carried = advance(steps + index - 1, carried, range(index, 4))

    half = SEQ // 2
    section = sec_ref[0]

    def keep(source, target):
        copy = pltpu.make_async_copy(source, target, copy_sem)
        copy.start()
        copy.wait()

    @pl.when(section == layer)
    def _():
        keep(xo_ref, own_ref)

    @pl.when(section == (layer - 1) % LAYERS)
    def _():
        keep(xo_ref.at[:half], far_ref.at[0])

    @pl.when(section == (layer + 1) % LAYERS)
    def _():
        keep(xo_ref.at[half:], far_ref.at[1])


def run_layer(layer, section, operands):
    first_layer = len(operands) == 2
    stream = jax.ShapeDtypeStruct((SEQ, BLOCK, HEAD), jnp.bfloat16)
    tile = pltpu.VMEM((STEP, BLOCK, HEAD), jnp.bfloat16)
    return pl.pallas_call(
        functools.partial(layer_kernel, layer, first_layer),
        in_specs=[SM, VM, VM] if first_layer else [SM, VM, VM, VM, ANY, ANY],
        out_specs=[VM, VM, ANY, ANY],
        out_shape=[
            stream,
            jax.ShapeDtypeStruct((SEQ, BLOCK), jnp.float32),
            stream,
            jax.ShapeDtypeStruct((2, SEQ // 2, BLOCK, HEAD), jnp.bfloat16),
        ],
        scratch_shapes=[
            pltpu.VMEM((BLOCK, BLOCK), jnp.float32),
            tile,
            tile,
            tile,
            pltpu.VMEM((STEP * BLOCK, HEAD), jnp.float32),
            pltpu.VMEM((STEP * BLOCK, HEAD), jnp.float32),
            pltpu.SemaphoreType.DMA,
        ],
        input_output_aliases={} if first_layer else {4: 2, 5: 3},
        compiler_params=pltpu.CompilerParams(vmem_limit_bytes=24 << 20),
        cost_estimate=pl.CostEstimate(flops=1_100_000_000, bytes_accessed=2 << 20, transcendentals=1 << 20),
    )(section, *operands)


def order_kernel(sec_ref, *refs):
    out_ref = refs[-1]
    for by in range(LAYERS):
        out_ref[lax.rem(sec_ref[0] + LAYERS - by, LAYERS)] = refs[by][...]


def order(section, pieces):
    return pl.pallas_call(
        order_kernel,
        in_specs=[SM] + [VM] * LAYERS,
        out_specs=VM,
        out_shape=jax.ShapeDtypeStruct((LAYERS,) + pieces[0].shape, pieces[0].dtype),
        compiler_params=pltpu.CompilerParams(vmem_limit_bytes=16 << 20),
    )(section, *pieces)


def gather_weights(section, own):
    up_two, down_two = around(own, 2), around(own, -2)
    up_one, down_one = around(own, 1), around(own, -1)
    up_four, up_three = around(up_two, 2), around(up_two, 1)
    down_three = around(down_two, -1)
    return order(section, [own, up_one, up_two, up_three, up_four, down_three, down_two, down_one])


def unpack_kernel(sec_ref, own_ref, other_ref, out_ref):
    micro = lax.rem(sec_ref[0], MICRO)
    for h in range(SEQ):
        out_ref[0, micro, :, h * HEAD : (h + 1) * HEAD] = own_ref[h]
        out_ref[0, 1 - micro, :, h * HEAD : (h + 1) * HEAD] = other_ref[h]


def unpack(section, own, other):
    return pl.pallas_call(
        unpack_kernel,
        in_specs=[SM, VM, VM],
        out_specs=VM,
        out_shape=jax.ShapeDtypeStruct((1, MICRO, BLOCK, WIDTH), jnp.bfloat16),
        compiler_params=pltpu.CompilerParams(vmem_limit_bytes=16 << 20),
    )(section, own, other)


def spread_sums(value):
    swap = [(i, i ^ 1) for i in range(SEQ)]
    value = value + lax.ppermute(value, "seq", swap)
    groups = [[2 * chip + core for chip in range(CHIPS)] for core in range(2)]
    copies = jnp.broadcast_to(value[None], (CHIPS,) + value.shape)
    return lax.all_to_all(copies, "seq", 0, 0, tiled=True, axis_index_groups=groups)


def around(value, by):
    sections = lax.axis_size("section")
    return lax.ppermute(value, "section", [(i, (i + by) % sections) for i in range(sections)])


def on_device(stream_in, norm_gain, proj_weight):
    head = lax.axis_index("seq")
    section = lax.axis_index("section").astype(jnp.int32).reshape(1)
    own_weights = prepare(head.astype(jnp.int32).reshape(1), proj_weight, norm_gain)
    weights = gather_weights(section, own_weights)

    x = lax.all_to_all(pack(section, stream_in), "seq", split_axis=0, concat_axis=0, tiled=True)
    x, sums, own, far = run_layer(0, section, (weights, x))
    for layer in range(1, LAYERS):
        x, sums, own, far = run_layer(layer, section, (spread_sums(sums), weights, x, own, far))
    low = around(far[0], 1)
    high = around(far[1], -1)
    own = lax.all_to_all(own, "seq", split_axis=0, concat_axis=0, tiled=True)
    other = lax.all_to_all(jnp.concatenate([low, high], axis=0), "seq", split_axis=0, concat_axis=0, tiled=True)
    return unpack(section, own, other)


def solution(mesh):
    in_specs = (P(None, "seq", None), P("section", None), P("section", None, None, None, None))
    out_specs = P("section", None, "seq", None)
    return jax.shard_map(on_device, mesh=mesh, in_specs=in_specs, out_specs=out_specs, check_vma=False)
```

```python
import functools

import jax
import jax.numpy as jnp
from jax import lax
from jax.experimental import pallas as pl
from jax.experimental.pallas import tpu as pltpu
from jax.sharding import PartitionSpec as P

epsilon = 1e-05
LAYERS = 8
SEQ = 32
MICRO = 2
BLOCK = 128
HEAD = 128
WIDTH = 4096
STEP = 4
EXTRA = 16
CHIPS = SEQ // 2
NT = (((1,), (1,)), ((), ()))
VM = pl.BlockSpec(memory_space=pltpu.VMEM)
SM = pl.BlockSpec(memory_space=pltpu.SMEM)
ANY = pl.BlockSpec(memory_space=pl.ANY)


def dot(a, b):
    return jnp.dot(a, b, preferred_element_type=jnp.float32)


def split_rows(row):
    high = row.astype(jnp.bfloat16)
    rest = row - high.astype(jnp.float32)
    middle = rest.astype(jnp.bfloat16)
    low = (rest - middle.astype(jnp.float32)).astype(jnp.bfloat16)
    rows = lax.broadcasted_iota(jnp.int32, (EXTRA, HEAD), 0)
    wide_rows = [jnp.broadcast_to(p.astype(jnp.float32), (EXTRA, HEAD)) for p in (high, middle, low)]
    tail = jnp.where(rows == 0, wide_rows[0], jnp.where(rows == 1, wide_rows[1], jnp.where(rows == 2, wide_rows[2], 0.0)))
    return tail.astype(jnp.bfloat16)


def split_squares(values):
    squares = values * values
    high = squares.astype(jnp.bfloat16)
    return jnp.concatenate([high, (squares - high.astype(jnp.float32)).astype(jnp.bfloat16)], axis=1)


def prepare_kernel(head_ref, weight_ref, gain_ref, out_ref, own_ref, copy_sem):
    head = head_ref[0]
    copy = pltpu.make_async_copy(weight_ref.at[0, head], own_ref, copy_sem)
    copy.start()
    gain = gain_ref[:, pl.ds(pl.multiple_of(head * HEAD, HEAD), HEAD)]
    out_ref[4 * HEAD :, :] = split_rows(gain)
    copy.wait()
    for n in range(4):
        piece = own_ref[n]
        if n == 1:
            piece = piece.astype(jnp.float32).T.astype(jnp.bfloat16)
        out_ref[n * HEAD : (n + 1) * HEAD, :] = piece


def prepare(head, proj_weight, norm_gain):
    return pl.pallas_call(
        prepare_kernel,
        in_specs=[SM, ANY, VM],
        out_specs=VM,
        out_shape=jax.ShapeDtypeStruct((4 * HEAD + EXTRA, HEAD), jnp.bfloat16),
        scratch_shapes=[pltpu.VMEM((4, HEAD, HEAD), jnp.bfloat16), pltpu.SemaphoreType.DMA],
        compiler_params=pltpu.CompilerParams(vmem_limit_bytes=16 << 20),
    )(head, proj_weight, norm_gain)


def pack_kernel(sec_ref, stream_ref, packed_ref, x_ref, copy_sem):
    copy = pltpu.make_async_copy(stream_ref.at[lax.rem(sec_ref[0], MICRO)], x_ref, copy_sem)
    copy.start()
    copy.wait()
    total = jnp.zeros((BLOCK, HEAD), jnp.float32)
    for h in range(SEQ):
        piece = x_ref[:, h * HEAD : (h + 1) * HEAD]
        packed_ref[h, :BLOCK, :] = piece
        wide = piece.astype(jnp.float32)
        total = total + wide * wide
    row = jnp.broadcast_to(jnp.sum(total, axis=1, keepdims=True), (BLOCK, HEAD)).T[:1]
    tail = split_rows(row)
    for h in range(SEQ):
        packed_ref[h, BLOCK:, :] = tail


def pack(section, stream):
    return pl.pallas_call(
        pack_kernel,
        in_specs=[SM, ANY],
        out_specs=VM,
        scratch_shapes=[pltpu.VMEM((BLOCK, WIDTH), jnp.bfloat16), pltpu.SemaphoreType.DMA],
        out_shape=jax.ShapeDtypeStruct((SEQ, BLOCK + EXTRA, HEAD), jnp.bfloat16),
        compiler_params=pltpu.CompilerParams(vmem_limit_bytes=16 << 20),
    )(section, stream)


def layer_kernel(layer, first_layer, sec_ref, *refs):
    sum_refs = () if first_layer else refs[:1]
    w_ref, x_ref = refs[len(sum_refs) : len(sum_refs) + 2]
    outputs = refs[2:] if first_layer else refs[5:]
    xo_ref, ss_ref, own_ref, far_ref, column_ref, q_ref, k_ref, v_ref, attn_ref, out_ref, copy_sem = outputs
    if first_layer:
        tail = x_ref[:, BLOCK:, :].astype(jnp.float32)
        total = tail[:, 0, :] + tail[:, 1, :] + tail[:, 2, :]
    else:
        total = sum_refs[0][0]
        for n in range(1, CHIPS):
            total = total + sum_refs[0][n]
    scale_rows = lax.rsqrt(total * (1.0 / WIDTH) + epsilon)
    column_ref[...] = jnp.concatenate([scale_rows] * (BLOCK // SEQ), axis=0).T
    wq, wk, wv, wo = [w_ref[layer, n * HEAD : (n + 1) * HEAD, :] for n in range(4)]
    wqv = jnp.concatenate([wq, wv], axis=1)
    gain_rows = w_ref[layer, 4 * HEAD :, :].astype(jnp.float32)
    gain = gain_rows[0:1] + gain_rows[1:2] + gain_rows[2:3]
    lanes = lax.broadcasted_iota(jnp.int32, (BLOCK, BLOCK), 1)
    rows = lax.broadcasted_iota(jnp.int32, (BLOCK, BLOCK), 0)
    causal = rows >= lanes
    ones_row = jnp.ones((8, 2 * HEAD), jnp.bfloat16)

    size = STEP * BLOCK

    def project(index):
        parts = []
        for n in range(STEP):
            block = index * STEP + n
            scale = jnp.sum(jnp.where(lanes == block, column_ref[...], 0.0), axis=1, keepdims=True)
            parts.append((x_ref[block, :BLOCK, :].astype(jnp.float32) * scale * gain).astype(jnp.bfloat16))
        normed = jnp.concatenate(parts, axis=0)
        return dot(normed, wqv), lax.dot_general(wk, normed, NT, preferred_element_type=jnp.float32)

    def activate(index, u, keys):
        for n in range(STEP):
            part = slice(n * BLOCK, (n + 1) * BLOCK)
            h = u[part, :HEAD] * 0.5
            q_ref[n] = (h * jnp.tanh(h) + h).astype(jnp.bfloat16)
            v_ref[n] = u[part, HEAD:].astype(jnp.bfloat16)
            h = keys[:, part] * 0.5
            k_ref[n] = (h * jnp.tanh(h) + h).astype(jnp.bfloat16)

    def finish(index):
        tile = pl.ds(index * STEP, STEP)
        x = x_ref[tile, :BLOCK, :].reshape(size, HEAD)
        new = (x.astype(jnp.float32) + out_ref[...]).astype(jnp.bfloat16)
        xo_ref[tile] = new.reshape(STEP, BLOCK, HEAD)
        wide = new.astype(jnp.float32)
        row = lax.dot_general(ones_row, split_squares(wide), NT, preferred_element_type=jnp.float32)
        for n in range(STEP):
            ss_ref[pl.ds(index * STEP + n, 1), :] = row[:1, n * BLOCK : (n + 1) * BLOCK]

    def advance(index, carried, stages):
        if 1 in stages:
            qs = [q_ref[n] for n in range(STEP)]
            ks = [k_ref[n] for n in range(STEP)]
            vs = [v_ref[n] for n in range(STEP)]
            scores = [jnp.where(causal, dot(qs[n], ks[n]), 0.0).astype(jnp.bfloat16) for n in range(STEP)]
        if 1 in stages:
            states = [dot(ks[n], vs[n]) for n in range(STEP)]
        if 2 in stages:
            attn = attn_ref[...]
            squares = jnp.sum(attn * attn, axis=1, keepdims=True)
        if 3 in stages:
            finish(index - 3)
        if 0 in stages:
            projected = project(index)
        if 1 in stages:
            for n in range(STEP):
                left = jnp.concatenate([scores[n], qs[n]], axis=1)
                part = dot(left, jnp.concatenate([vs[n], carried.astype(jnp.bfloat16)], axis=0))
                attn_ref[n * BLOCK : (n + 1) * BLOCK, :] = part
                carried = carried + states[n]
        if 2 in stages:
            scale = lax.rsqrt(squares * (1.0 / HEAD) + epsilon)
            out_ref[...] = dot((attn * scale).astype(jnp.bfloat16), wo)
        if 0 in stages:
            activate(index, *projected)
        return carried

    steps = SEQ // STEP
    carried = jnp.zeros((HEAD, HEAD), jnp.float32)
    for index in range(3):
        carried = advance(index, carried, range(index + 1))
    carried = lax.fori_loop(3, steps, lambda i, c: advance(i, c, range(4)), carried)
    for index in range(1, 4):
        carried = advance(steps + index - 1, carried, range(index, 4))

    half = SEQ // 2
    section = sec_ref[0]

    def keep(source, target):
        copy = pltpu.make_async_copy(source, target, copy_sem)
        copy.start()
        copy.wait()

    @pl.when(section == layer)
    def _():
        keep(xo_ref, own_ref)

    @pl.when(section == (layer - 1) % LAYERS)
    def _():
        keep(xo_ref.at[:half], far_ref.at[0])

    @pl.when(section == (layer + 1) % LAYERS)
    def _():
        keep(xo_ref.at[half:], far_ref.at[1])


def run_layer(layer, section, operands):
    first_layer = len(operands) == 2
    stream = jax.ShapeDtypeStruct((SEQ, BLOCK, HEAD), jnp.bfloat16)
    tile = pltpu.VMEM((STEP, BLOCK, HEAD), jnp.bfloat16)
    return pl.pallas_call(
        functools.partial(layer_kernel, layer, first_layer),
        in_specs=[SM, VM, VM] if first_layer else [SM, VM, VM, VM, ANY, ANY],
        out_specs=[VM, VM, ANY, ANY],
        out_shape=[
            stream,
            jax.ShapeDtypeStruct((SEQ, BLOCK), jnp.float32),
            stream,
            jax.ShapeDtypeStruct((2, SEQ // 2, BLOCK, HEAD), jnp.bfloat16),
        ],
        scratch_shapes=[
            pltpu.VMEM((BLOCK, BLOCK), jnp.float32),
            tile,
            tile,
            tile,
            pltpu.VMEM((STEP * BLOCK, HEAD), jnp.float32),
            pltpu.VMEM((STEP * BLOCK, HEAD), jnp.float32),
            pltpu.SemaphoreType.DMA,
        ],
        input_output_aliases={} if first_layer else {4: 2, 5: 3},
        compiler_params=pltpu.CompilerParams(vmem_limit_bytes=24 << 20),
        cost_estimate=pl.CostEstimate(flops=1_100_000_000, bytes_accessed=2 << 20, transcendentals=1 << 20),
    )(section, *operands)


def order_kernel(sec_ref, *refs):
    out_ref = refs[-1]
    for by in range(LAYERS):
        out_ref[lax.rem(sec_ref[0] + LAYERS - by, LAYERS)] = refs[by][...]


def order(section, pieces):
    return pl.pallas_call(
        order_kernel,
        in_specs=[SM] + [VM] * LAYERS,
        out_specs=VM,
        out_shape=jax.ShapeDtypeStruct((LAYERS,) + pieces[0].shape, pieces[0].dtype),
        compiler_params=pltpu.CompilerParams(vmem_limit_bytes=16 << 20),
    )(section, *pieces)


def gather_weights(section, own):
    up_two, down_two = around(own, 2), around(own, -2)
    up_one, down_one = around(own, 1), around(own, -1)
    far_up, far_down = around(up_two[:256], 2), around(down_two[256:], -2)
    up_three, down_three = around(up_two, 1), around(down_two, -1)
    up_four = jnp.concatenate([far_up, far_down], axis=0)
    return order(section, [own, up_one, up_two, up_three, up_four, down_three, down_two, down_one])


def unpack_kernel(sec_ref, own_ref, other_ref, out_ref):
    micro = lax.rem(sec_ref[0], MICRO)
    for h in range(SEQ):
        out_ref[0, micro, :, h * HEAD : (h + 1) * HEAD] = own_ref[h]
        out_ref[0, 1 - micro, :, h * HEAD : (h + 1) * HEAD] = other_ref[h]


def unpack(section, own, other):
    return pl.pallas_call(
        unpack_kernel,
        in_specs=[SM, VM, VM],
        out_specs=VM,
        out_shape=jax.ShapeDtypeStruct((1, MICRO, BLOCK, WIDTH), jnp.bfloat16),
        compiler_params=pltpu.CompilerParams(vmem_limit_bytes=16 << 20),
    )(section, own, other)


def spread_sums(value):
    swap = [(i, i ^ 1) for i in range(SEQ)]
    value = value + lax.ppermute(value, "seq", swap)
    groups = [[2 * chip + core for chip in range(CHIPS)] for core in range(2)]
    copies = jnp.broadcast_to(value[None], (CHIPS,) + value.shape)
    return lax.all_to_all(copies, "seq", 0, 0, tiled=True, axis_index_groups=groups)


def around(value, by):
    sections = lax.axis_size("section")
    return lax.ppermute(value, "section", [(i, (i + by) % sections) for i in range(sections)])


def on_device(stream_in, norm_gain, proj_weight):
    head = lax.axis_index("seq")
    section = lax.axis_index("section").astype(jnp.int32).reshape(1)
    own_weights = prepare(head.astype(jnp.int32).reshape(1), proj_weight, norm_gain)
    weights = gather_weights(section, own_weights)

    x = lax.all_to_all(pack(section, stream_in), "seq", split_axis=0, concat_axis=0, tiled=True)
    x, sums, own, far = run_layer(0, section, (weights, x))
    for layer in range(1, LAYERS):
        x, sums, own, far = run_layer(layer, section, (spread_sums(sums), weights, x, own, far))
    low = around(far[0], 1)
    high = around(far[1], -1)
    own = lax.all_to_all(own, "seq", split_axis=0, concat_axis=0, tiled=True)
    other = lax.all_to_all(jnp.concatenate([low, high], axis=0), "seq", split_axis=0, concat_axis=0, tiled=True)
    return unpack(section, own, other)


def solution(mesh):
    in_specs = (P(None, "seq", None), P("section", None), P("section", None, None, None, None))
    out_specs = P("section", None, "seq", None)
    return jax.shard_map(on_device, mesh=mesh, in_specs=in_specs, out_specs=out_specs, check_vma=False)
```
